32 devices in a mesh: dp: 8 (over z, x), tensor: 4 (over y, core).
Axes of the slice: x: 2, y: 2, z: 4, core: 2. Of those that a mesh axis runs over, the one named last changes fastest.
Arguments:
- tokens: bfloat16 [16, 512, 1024], P('dp'), may hold values from -6 to 6
- out_grad: bfloat16 [16, 512, 1024], P('dp'), may hold values from -6 to 6
- first_gain: float32 [1024], replicated, may hold values from 0.5 to 1.5
- query_weight: bfloat16 [1024, 2048], P(None, 'tensor'), may hold values from -0.1875 to 0.1875
- key_weight: bfloat16 [1024, 2048], P(None, 'tensor'), may hold values from -0.1875 to 0.1875
- value_weight: bfloat16 [1024, 4096], P(None, 'tensor'), may hold values from -0.1875 to 0.1875
- gate_weight: bfloat16 [1024, 4096], P(None, 'tensor'), may hold values from -0.1875 to 0.1875
- beta_weight: bfloat16 [1024, 16], P(None, 'tensor'), may hold values from -0.1875 to 0.1875
- decay_weight: bfloat16 [1024, 16], P(None, 'tensor'), may hold values from -0.1875 to 0.1875
- query_filter: bfloat16 [4, 2048], P(None, 'tensor'), may hold values from -3 to 3
- key_filter: bfloat16 [4, 2048], P(None, 'tensor'), may hold values from -3 to 3
- value_filter: bfloat16 [4, 4096], P(None, 'tensor'), may hold values from -3 to 3
- decay_log: float32 [16], P('tensor'), may hold values from -1.5 to 2.5
- decay_bias: float32 [16], P('tensor'), may hold values from -6 to -2
- mixer_gain: float32 [256], replicated, may hold values from 0.5 to 1.5
- out_weight: bfloat16 [1024, 4096], P(None, 'tensor'), may hold values from -0.125 to 0.125
- second_gain: float32 [1024], replicated, may hold values from 0.5 to 1.5
- ffn_gate_weight: bfloat16 [1024, 2816], P(None, 'tensor'), may hold values from -0.1875 to 0.1875
- ffn_up_weight: bfloat16 [1024, 2816], P(None, 'tensor'), may hold values from -0.1875 to 0.1875
- ffn_down_weight: bfloat16 [1024, 2816], P(None, 'tensor'), may hold values from -0.15625 to 0.15625
Outputs:
- output: bfloat16 [16, 512, 1024], P('dp')
- tokens_grad: bfloat16 [16, 512, 1024], P('dp')
- grad_first_gain: float32 [1024], replicated
- grad_query_weight: float32 [1024, 2048], P(None, 'tensor')
- grad_key_weight: float32 [1024, 2048], P(None, 'tensor')
- grad_value_weight: float32 [1024, 4096], P(None, 'tensor')
- grad_gate_weight: float32 [1024, 4096], P(None, 'tensor')
- grad_beta_weight: float32 [1024, 16], P(None, 'tensor')
- grad_decay_weight: float32 [1024, 16], P(None, 'tensor')
- grad_query_filter: float32 [4, 2048], P(None, 'tensor')
- grad_key_filter: float32 [4, 2048], P(None, 'tensor')
- grad_value_filter: float32 [4, 4096], P(None, 'tensor')
- grad_decay_log: float32 [16], P('tensor')
- grad_decay_bias: float32 [16], P('tensor')
- grad_mixer_gain: float32 [256], replicated
- grad_out_weight: float32 [1024, 4096], P(None, 'tensor')
- grad_second_gain: float32 [1024], replicated
- grad_ffn_gate_weight: float32 [1024, 2816], P(None, 'tensor')
- grad_ffn_up_weight: float32 [1024, 2816], P(None, 'tensor')
- grad_ffn_down_weight: float32 [1024, 2816], P(None, 'tensor')
The draws below stay inside these ranges and needn't reach their ends.
All inputs are finite; a program needn't handle non-finite values.
Results may differ from the reference program's by a relative error of at most 0.018.
Values sent between devices are 32-bit elements; how exact they have to be, the bound alone decides.
No kernel may reach another device: no remote copies, remote signals or barrier semaphores. Data moves between devices by JAX's collectives and lax.ppermute only.
A program may use at most 320 MiB of HBM per device.

```python
import jax
import jax.numpy as jnp
from jax import lax

D = 1024
H = 16
DK = 128
DV = 256
FF = 2816
CONV = 4
STRETCH = 64
SEQ = 512
MICRO = 2
BATCH = 16


def block_scale(rng, dims, pieces, low, high):
    factor_of = 1.0
    for dim, blocks in pieces:
        draws = jax.random.uniform(jax.random.fold_in(jax.random.fold_in(rng, 6), dim), (blocks,), jnp.float32, low / len(pieces), high / len(pieces))
        factor_of = factor_of * jnp.repeat(jnp.exp(draws), dims[dim] // blocks).reshape((-1,) + (1,) * (len(dims) - 1 - dim))
    return factor_of


def scatter_about(own_key, dims, scale, bound, cuts=(), kind=jnp.bfloat16):
    factor_of = block_scale(own_key, dims, cuts, -0.22, 0.18) if cuts else 1.0
    values = jax.random.normal(own_key, dims, jnp.float32) * scale * factor_of
    return jnp.minimum(jnp.maximum(values, -bound), bound).astype(kind)


def setup_inputs(seed: int = 0) -> dict:
    arg_keys = jax.random.split(jax.random.key(seed), 21)
    tokens = scatter_about(arg_keys[0], (BATCH, SEQ, D), 1.0, 6.0, ((0, 8),))
    out_grad = scatter_about(arg_keys[1], (BATCH, SEQ, D), 1.0, 6.0, ((0, 8),))
    first_gain = jnp.clip(1.0 + 0.1 * jax.random.normal(arg_keys[2], (D,), jnp.float32), 0.5, 1.5)
    query_weight = scatter_about(arg_keys[3], (D, H * DK), D ** -0.5, 0.1875, ((1, 4),))
    key_weight = scatter_about(arg_keys[4], (D, H * DK), D ** -0.5, 0.1875, ((1, 4),))
    value_weight = scatter_about(arg_keys[5], (D, H * DV), D ** -0.5, 0.1875, ((1, 4),))
    gate_weight = scatter_about(arg_keys[6], (D, H * DV), D ** -0.5, 0.1875, ((1, 4),))
    beta_weight = scatter_about(arg_keys[7], (D, H), D ** -0.5, 0.1875, ((1, 4),))
    decay_weight = scatter_about(arg_keys[8], (D, H), D ** -0.5, 0.1875, ((1, 4),))
    query_filter = scatter_about(arg_keys[9], (CONV, H * DK), CONV ** -0.5, 3.0, ((1, 4),))
    key_filter = scatter_about(arg_keys[10], (CONV, H * DK), CONV ** -0.5, 3.0, ((1, 4),))
    value_filter = scatter_about(arg_keys[11], (CONV, H * DV), CONV ** -0.5, 3.0, ((1, 4),))
    decay_log = jnp.clip(-1.5 + 4.0 * jax.random.uniform(arg_keys[12], (H,), jnp.float32) ** block_scale(arg_keys[12], (H,), ((0, 4),), -0.2, 0.2), -1.5, 2.5)
    decay_bias = jnp.clip(-6.0 + 4.0 * jax.random.uniform(arg_keys[13], (H,), jnp.float32) ** block_scale(arg_keys[13], (H,), ((0, 4),), -0.2, 0.2), -6.0, -2.0)
    mixer_gain = jnp.clip(1.0 + 0.1 * jax.random.normal(arg_keys[14], (DV,), jnp.float32), 0.5, 1.5)
    out_weight = scatter_about(arg_keys[15], (D, H * DV), (H * DV // 2) ** -0.5, 0.125, ((1, 4),))
    second_gain = jnp.clip(1.0 + 0.1 * jax.random.normal(arg_keys[16], (D,), jnp.float32), 0.5, 1.5)
    ffn_gate_weight = scatter_about(arg_keys[17], (D, FF), D ** -0.5, 0.1875, ((1, 4),))
    ffn_up_weight = scatter_about(arg_keys[18], (D, FF), D ** -0.5, 0.1875, ((1, 4),))
    ffn_down_weight = scatter_about(arg_keys[19], (D, FF), (FF // 2) ** -0.5, 0.15625, ((1, 4),))
    return dict(tokens=tokens, out_grad=out_grad, first_gain=first_gain, query_weight=query_weight, key_weight=key_weight, value_weight=value_weight, gate_weight=gate_weight, beta_weight=beta_weight, decay_weight=decay_weight, query_filter=query_filter, key_filter=key_filter, value_filter=value_filter, decay_log=decay_log, decay_bias=decay_bias, mixer_gain=mixer_gain, out_weight=out_weight, second_gain=second_gain, ffn_gate_weight=ffn_gate_weight, ffn_up_weight=ffn_up_weight, ffn_down_weight=ffn_down_weight)


HIGHEST = lax.Precision.HIGHEST
EPSILON = 1e-06

@jax.custom_vjp
def low(v):
    return lax.optimization_barrier(v.astype(jnp.bfloat16)).astype(jnp.float32)

@jax.custom_vjp
def low_back(v):
    return v

def low_keep(v):
    return (low(v), None)

def low_pass(kept, grad):
    return (grad,)

def back_keep(v):
    return (v, None)

def back_low(kept, grad):
    return (low(grad),)
low.defvjp(low_keep, low_pass)
low_back.defvjp(back_keep, back_low)

def root_norm(values, gain):
    return values * lax.rsqrt(lax.optimization_barrier(jnp.mean(values * values, -1, keepdims=True)) + EPSILON) * gain

def short_filter(raw, taps):
    width = taps.shape[0]
    length = raw.shape[1]
    padded = jnp.pad(raw, ((0, 0), (width - 1, 0), (0, 0)))
    total = taps[0] * padded[:, 0:length, :]
    for offset in range(1, width):
        total = total + taps[offset] * padded[:, offset:offset + length, :]
    return jax.nn.silu(total)

def unit_rows(values, heads):
    batch, length, channels = values.shape
    split = values.reshape(batch, length, heads, channels // heads)
    return split * lax.rsqrt(lax.optimization_barrier(jnp.sum(split * split, -1, keepdims=True)) + EPSILON)

def prepare(query_raw, key_raw, value_raw, query_filter, key_filter, value_filter):
    heads = query_raw.shape[-1] // DK
    batch, length = (query_raw.shape[0], query_raw.shape[1])
    query = unit_rows(short_filter(query_raw, query_filter), heads) * DK ** (-0.5)
    key = unit_rows(short_filter(key_raw, key_filter), heads)
    value = short_filter(value_raw, value_filter).reshape(batch, length, heads, DV)
    return (query, key, value)

def decay_gates(beta_raw, decay_raw, decay_log, decay_bias):
    return (jax.nn.sigmoid(beta_raw), -jnp.exp(decay_log) * jax.nn.softplus(decay_raw + decay_bias))

def output_norm(mixed, gate_raw, gain):
    batch, length, heads, width = mixed.shape
    gated = jax.nn.silu(gate_raw.reshape(batch, length, heads, width))
    return (root_norm(mixed, gain) * gated).reshape(batch, length, heads * width)

def swiglu(gate, upward):
    return jax.nn.silu(gate) * upward

def delta_rule(query, key, value, beta, logdecay):
    batch, length, heads, kdim = query.shape
    vdim = value.shape[-1]
    blocks = length // STRETCH

    def to_blocks(array):
        shaped = array.reshape((batch, blocks, STRETCH, heads) + array.shape[3:])
        return jnp.swapaxes(shaped, 2, 3)
    query_blocks = to_blocks(query)
    key_blocks = to_blocks(key)
    value_blocks = to_blocks(value)
    beta_blocks = to_blocks(beta)
    cumulative = jnp.cumsum(to_blocks(logdecay), -1)
    rows = lax.broadcasted_iota(jnp.int32, (STRETCH, STRETCH), 0)
    cols = lax.broadcasted_iota(jnp.int32, (STRETCH, STRETCH), 1)
    strict = rows > cols
    inclusive = rows >= cols
    spread = cumulative[..., :, None] - cumulative[..., None, :]
    decay = jnp.where(inclusive, jnp.exp(jnp.where(inclusive, spread, 0.0)), 0.0)
    intersection = jnp.einsum('bnhik,bnhjk->bnhij', key_blocks, key_blocks, precision=HIGHEST)
    lower = jnp.where(strict, beta_blocks[..., :, None] * intersection * decay, 0.0)
    identity = jnp.eye(STRETCH, dtype=jnp.float32)
    inverse = identity - lower
    power = lower
    span = 2
    while span < STRETCH:
        power = jnp.einsum('bnhij,bnhjk->bnhik', power, power, precision=HIGHEST)
        inverse = jnp.einsum('bnhij,bnhjk->bnhik', inverse, identity + power, precision=HIGHEST)
        span = span * 2
    key_scaled = (beta_blocks * jnp.exp(cumulative))[..., None] * key_blocks
    key_mix = jnp.einsum('bnhij,bnhjk->bnhik', inverse, key_scaled, precision=HIGHEST)
    value_mix = jnp.einsum('bnhij,bnhjv->bnhiv', inverse, beta_blocks[..., None] * value_blocks, precision=HIGHEST)
    scores = jnp.einsum('bnhik,bnhjk->bnhij', query_blocks, key_blocks, precision=HIGHEST) * decay
    query_decayed = query_blocks * jnp.exp(cumulative)[..., None]
    key_decayed = key_blocks * jnp.exp(cumulative[..., -1:] - cumulative)[..., None]
    tail = jnp.exp(cumulative[..., -1])
    parts = tuple((jnp.moveaxis(piece, 1, 0) for piece in (key_mix, value_mix, query_decayed, scores, key_decayed, tail)))

    def advance(state, part):
        mix_keys, mix_values, decayed_queries, block_scores, decayed_keys, block_tail = part
        fresh = mix_values - jnp.einsum('bhck,bhkv->bhcv', mix_keys, state, precision=HIGHEST)
        result = jnp.einsum('bhck,bhkv->bhcv', decayed_queries, state, precision=HIGHEST)
        result = result + jnp.einsum('bhij,bhjv->bhiv', block_scores, fresh, precision=HIGHEST)
        state = block_tail[..., None, None] * state + jnp.einsum('bhck,bhcv->bhkv', decayed_keys, fresh, precision=HIGHEST)
        return (state, result)
    start = jnp.zeros((batch, heads, kdim, vdim), jnp.float32)
    finish, results = lax.scan(jax.checkpoint(advance), start, parts)
    results = jnp.transpose(results, (1, 0, 3, 2, 4))
    return results.reshape(batch, length, heads, vdim)

def project(left, right):
    return jnp.einsum('bsd,df->bsf', left, right, precision=HIGHEST)

def back_project(left, right):
    return jnp.einsum('bsf,df->bsd', left, right, precision=HIGHEST)

def layer(params, inputs):
    first_gain, query_weight, key_weight, value_weight, gate_weight, beta_weight, decay_weight, query_filter, key_filter, value_filter, decay_log, decay_bias, mixer_gain, out_weight, second_gain, ffn_gate_weight, ffn_up_weight, ffn_down_weight = params
    first_normed = low(root_norm(inputs, first_gain))
    query_raw = low_back(project(first_normed, query_weight))
    key_raw = low_back(project(first_normed, key_weight))
    value_raw = low_back(project(first_normed, value_weight))
    gate_raw = low_back(project(first_normed, gate_weight))
    beta_raw = low_back(project(first_normed, beta_weight))
    decay_raw = low_back(project(first_normed, decay_weight))
    query, key, value = prepare(query_raw, key_raw, value_raw, query_filter, key_filter, value_filter)
    query = low(low_back(query))
    key = low(low_back(key))
    value = low(low_back(value))
    beta, logdecay = decay_gates(beta_raw, decay_raw, decay_log, decay_bias)
    mixed = delta_rule(query, key, value, beta, logdecay)
    mixer_out = low(output_norm(mixed, gate_raw, mixer_gain))
    mixer_sum = low_back(back_project(mixer_out, out_weight))
    middle = inputs + mixer_sum
    second_normed = low(root_norm(middle, second_gain))
    ffn_gate = low_back(project(second_normed, ffn_gate_weight))
    ffn_up = low_back(project(second_normed, ffn_up_weight))
    hidden = low(swiglu(ffn_gate, ffn_up))
    ffn_sum = low_back(back_project(hidden, ffn_down_weight))
    return middle + ffn_sum

def reference(tokens, out_grad, first_gain, query_weight, key_weight, value_weight, gate_weight, beta_weight, decay_weight, query_filter, key_filter, value_filter, decay_log, decay_bias, mixer_gain, out_weight, second_gain, ffn_gate_weight, ffn_up_weight, ffn_down_weight):
    params = tuple((weight.astype(jnp.float32) for weight in (first_gain, query_weight, key_weight, value_weight, gate_weight, beta_weight, decay_weight, query_filter, key_filter, value_filter, decay_log, decay_bias, mixer_gain, out_weight, second_gain, ffn_gate_weight, ffn_up_weight, ffn_down_weight)))
    groups = BATCH // MICRO
    inputs = tokens.astype(jnp.float32).reshape(groups, MICRO, SEQ, D)
    cotangent = out_grad.astype(jnp.float32).reshape(groups, MICRO, SEQ, D)

    def one_group(totals, pair):
        group_inputs, group_cotangent = pair
        result, pullback = jax.vjp(layer, params, group_inputs)
        grads, input_grad = pullback(group_cotangent)
        totals = jax.tree.map(jnp.add, totals, grads)
        return (totals, (result.astype(jnp.bfloat16), input_grad.astype(jnp.bfloat16)))
    start = jax.tree.map(jnp.zeros_like, params)
    totals, (results, input_grads) = lax.scan(one_group, start, (inputs, cotangent))
    return (results.reshape(BATCH, SEQ, D), input_grads.reshape(BATCH, SEQ, D), totals[0], totals[1], totals[2], totals[3], totals[4], totals[5], totals[6], totals[7], totals[8], totals[9], totals[10], totals[11], totals[12], totals[13], totals[14], totals[15], totals[16], totals[17])
```

```python
import jax
import jax.numpy as jnp
from jax import lax
from jax.sharding import PartitionSpec as P

DK = 128
DV = 256
STRETCH = 64


PRECISE = lax.Precision.HIGH
EPSILON = 1e-06


def root_norm(values, gain):
    return values * lax.rsqrt(jnp.mean(values * values, -1, keepdims=True) + EPSILON) * gain


def short_filter(raw, taps):
    width = taps.shape[0]
    length = raw.shape[1]
    padded = jnp.pad(raw, ((0, 0), (width - 1, 0), (0, 0)))
    total = taps[0] * padded[:, 0:length, :]
    for offset in range(1, width):
        total = total + taps[offset] * padded[:, offset : offset + length, :]
    return jax.nn.silu(total)


def unit_rows(values, heads):
    batch, length, channels = values.shape
    split = values.reshape(batch, length, heads, channels // heads)
    return split * lax.rsqrt(jnp.sum(split * split, -1, keepdims=True) + EPSILON)


def prepare(query_raw, key_raw, value_raw, query_filter, key_filter, value_filter):
    heads = query_raw.shape[-1] // DK
    batch, length = (query_raw.shape[0], query_raw.shape[1])
    query = unit_rows(short_filter(query_raw, query_filter), heads) * DK ** (-0.5)
    key = unit_rows(short_filter(key_raw, key_filter), heads)
    value = short_filter(value_raw, value_filter).reshape(batch, length, heads, DV)
    return (query, key, value)


def decay_gates(beta_raw, decay_raw, decay_log, decay_bias):
    return (jax.nn.sigmoid(beta_raw), -jnp.exp(decay_log) * jax.nn.softplus(decay_raw + decay_bias))


def output_norm(mixed, gate_raw, gain):
    batch, length, heads, width = mixed.shape
    gated = jax.nn.silu(gate_raw.reshape(batch, length, heads, width))
    return (root_norm(mixed, gain) * gated).reshape(batch, length, heads * width)


def swiglu(gate, upward):
    return jax.nn.silu(gate) * upward


def delta_rule(query, key, value, beta, logdecay):
    batch, length, heads, kdim = query.shape
    vdim = value.shape[-1]
    blocks = length // STRETCH

    def to_blocks(array):
        shaped = array.reshape((batch, blocks, STRETCH, heads) + array.shape[3:])
        return jnp.swapaxes(shaped, 2, 3)

    query_blocks = to_blocks(query)
    key_blocks = to_blocks(key)
    value_blocks = to_blocks(value)
    beta_blocks = to_blocks(beta)
    cumulative = jnp.cumsum(to_blocks(logdecay), -1)
    rows = lax.broadcasted_iota(jnp.int32, (STRETCH, STRETCH), 0)
    cols = lax.broadcasted_iota(jnp.int32, (STRETCH, STRETCH), 1)
    strict = rows > cols
    inclusive = rows >= cols
    spread = cumulative[..., :, None] - cumulative[..., None, :]
    decay = jnp.where(inclusive, jnp.exp(jnp.where(inclusive, spread, 0.0)), 0.0)
    intersection = jnp.einsum("bnhik,bnhjk->bnhij", key_blocks, key_blocks, precision=PRECISE)
    lower = jnp.where(strict, beta_blocks[..., :, None] * intersection * decay, 0.0)
    identity = jnp.eye(STRETCH, dtype=jnp.float32)
    inverse = identity - lower
    power = lower
    span = 2
    while span < STRETCH:
        power = jnp.einsum("bnhij,bnhjk->bnhik", power, power, precision=PRECISE)
        inverse = jnp.einsum("bnhij,bnhjk->bnhik", inverse, identity + power, precision=PRECISE)
        span = span * 2
    key_scaled = (beta_blocks * jnp.exp(cumulative))[..., None] * key_blocks
    key_mix = jnp.einsum("bnhij,bnhjk->bnhik", inverse, key_scaled, precision=PRECISE)
    value_mix = jnp.einsum(
        "bnhij,bnhjv->bnhiv", inverse, beta_blocks[..., None] * value_blocks, precision=PRECISE
    )
    scores = jnp.einsum("bnhik,bnhjk->bnhij", query_blocks, key_blocks, precision=PRECISE) * decay
    query_decayed = query_blocks * jnp.exp(cumulative)[..., None]
    key_decayed = key_blocks * jnp.exp(cumulative[..., -1:] - cumulative)[..., None]
    tail = jnp.exp(cumulative[..., -1])
    parts = tuple(
        (
            jnp.moveaxis(piece, 1, 0)
            for piece in (key_mix, value_mix, query_decayed, scores, key_decayed, tail)
        )
    )

    def advance(state, part):
        mix_keys, mix_values, decayed_queries, block_scores, decayed_keys, block_tail = part
        fresh = mix_values - jnp.einsum("bhck,bhkv->bhcv", mix_keys, state, precision=PRECISE)
        result = jnp.einsum("bhck,bhkv->bhcv", decayed_queries, state, precision=PRECISE)
        result = result + jnp.einsum("bhij,bhjv->bhiv", block_scores, fresh, precision=PRECISE)
        state = block_tail[..., None, None] * state + jnp.einsum(
            "bhck,bhcv->bhkv", decayed_keys, fresh, precision=PRECISE
        )
        return (state, result)

    start = jnp.zeros((batch, heads, kdim, vdim), jnp.float32)
    finish, results = lax.scan(jax.checkpoint(advance), start, parts)
    results = jnp.transpose(results, (1, 0, 3, 2, 4))
    return results.reshape(batch, length, heads, vdim)


def matmul(left, right):
    return jnp.dot(left, right, preferred_element_type=jnp.float32)


def against_rows(left, right):
    return lax.dot_general(
        left, right, (((0,), (0,)), ((), ())), preferred_element_type=jnp.float32
    )


def against_cols(left, right):
    return lax.dot_general(
        left, right, (((1,), (1,)), ((), ())), preferred_element_type=jnp.float32
    )


def rounded_copy(values):
    return lax.optimization_barrier(values.astype(jnp.bfloat16)).astype(jnp.float32)


def swap_pairs(size, bit):
    return [(index, index ^ (1 << bit)) for index in range(size)]


def bits_of(size):
    return list(range(size.bit_length() - 1))


def halve(values, axis, bit):
    size = lax.axis_size(axis)
    upper = (lax.axis_index(axis) >> bit) & 1
    half = values.shape[0] // 2
    kept = lax.dynamic_slice_in_dim(values, upper * half, half, 0)
    given = lax.dynamic_slice_in_dim(values, (1 - upper) * half, half, 0)
    return kept + lax.ppermute(given, axis, swap_pairs(size, bit))


def double(values, axis, bit):
    size = lax.axis_size(axis)
    upper = (lax.axis_index(axis) >> bit) & 1
    other = lax.ppermute(values, axis, swap_pairs(size, bit))
    half = values.shape[0]
    whole = jnp.zeros((2 * half,) + values.shape[1:], values.dtype)
    whole = lax.dynamic_update_slice_in_dim(whole, values, upper * half, 0)
    return lax.dynamic_update_slice_in_dim(whole, other, (1 - upper) * half, 0)


def sum_by_halves(values, axis, order):
    for bit in order:
        values = halve(values, axis, bit)
    for bit in reversed(order):
        values = double(values, axis, bit)
    return values


def sum_whole(values, axis):
    size = lax.axis_size(axis)
    for bit in bits_of(size):
        values = values + lax.ppermute(values, axis, swap_pairs(size, bit))
    return values


def sum_tensor(values):
    size = lax.axis_size("tensor")
    values = halve(values, "tensor", 0)
    for bit in bits_of(size)[1:]:
        values = values + lax.ppermute(values, "tensor", swap_pairs(size, bit))
    return double(values, "tensor", 0)


def sum_dp(values):
    size = lax.axis_size("dp")
    ascending = bits_of(size)
    swapped = [1, 0] + ascending[2:]
    rows = values.shape[0]
    cut = (rows * 5 // 8)
    first = sum_by_halves(values[:cut], "dp", ascending)
    second = sum_by_halves(values[cut:], "dp", swapped)
    return jnp.concatenate([first, second], 0)


def body(
    tokens,
    out_grad,
    first_gain,
    query_weight,
    key_weight,
    value_weight,
    gate_weight,
    beta_weight,
    decay_weight,
    query_filter,
    key_filter,
    value_filter,
    decay_log,
    decay_bias,
    mixer_gain,
    out_weight,
    second_gain,
    ffn_gate_weight,
    ffn_up_weight,
    ffn_down_weight,
):
    weights_in = (query_weight, key_weight, value_weight, gate_weight, beta_weight, decay_weight)
    filters = (
        query_filter.astype(jnp.float32),
        key_filter.astype(jnp.float32),
        value_filter.astype(jnp.float32),
    )
    small_shapes = (
        query_filter.shape,
        key_filter.shape,
        value_filter.shape,
        decay_log.shape,
        decay_bias.shape,
        mixer_gain.shape,
        first_gain.shape,
        second_gain.shape,
    )
    totals = None
    outputs = []
    input_grads = []
    for index in range(tokens.shape[0]):
        inputs = tokens[index].astype(jnp.float32)
        first_float, pull_first = jax.vjp(root_norm, inputs, first_gain)
        first_normed = first_float.astype(jnp.bfloat16)
        raws = [matmul(first_normed, weight) for weight in weights_in]
        prepared, pull_prepare = jax.vjp(
            prepare, raws[0][None], raws[1][None], raws[2][None], filters[0], filters[1], filters[2]
        )
        query = prepared[0].astype(jnp.bfloat16)
        key = prepared[1].astype(jnp.bfloat16)
        value = prepared[2].astype(jnp.bfloat16)
        gated, pull_gates = jax.vjp(
            decay_gates, raws[4][None], raws[5][None], decay_log, decay_bias
        )
        mixed, pull_mix = jax.vjp(
            delta_rule,
            query.astype(jnp.float32),
            key.astype(jnp.float32),
            value.astype(jnp.float32),
            gated[0],
            gated[1],
        )
        mixer_float, pull_out = jax.vjp(output_norm, mixed, raws[3][None], mixer_gain)
        mixer_out = mixer_float[0].astype(jnp.bfloat16)
        mixer_sum = sum_tensor(against_cols(mixer_out, out_weight))
        middle = inputs + mixer_sum
        second_float, pull_second = jax.vjp(root_norm, middle, second_gain)
        second_normed = second_float.astype(jnp.bfloat16)
        ffn_gate = matmul(second_normed, ffn_gate_weight)
        ffn_up = matmul(second_normed, ffn_up_weight)
        hidden_float, pull_swiglu = jax.vjp(swiglu, ffn_gate, ffn_up)
        hidden = hidden_float.astype(jnp.bfloat16)
        ffn_sum = sum_tensor(against_cols(hidden, ffn_down_weight))
        outputs.append((middle + ffn_sum).astype(jnp.bfloat16))
        upstream = out_grad[index].astype(jnp.float32)
        ffn_back = out_grad[index]
        grad_down = against_rows(ffn_back, hidden)
        hidden_grad = matmul(ffn_back, ffn_down_weight)
        gate_grad, up_grad = pull_swiglu(hidden_grad)
        gate_back = gate_grad.astype(jnp.bfloat16)
        up_back = up_grad.astype(jnp.bfloat16)
        grad_fgate = against_rows(second_normed, gate_back)
        grad_fup = against_rows(second_normed, up_back)
        second_partial = against_cols(gate_back, ffn_gate_weight) + against_cols(
            up_back, ffn_up_weight
        )
        second_grad = sum_tensor(second_partial)
        middle_part, grad_second = pull_second(second_grad)
        middle_grad = upstream + middle_part
        mixer_back = middle_grad.astype(jnp.bfloat16)
        grad_out = against_rows(mixer_back, mixer_out)
        outnorm_grad = matmul(mixer_back, out_weight)
        mixed_grad, gate_raw_grad, mixer_gain_part = pull_out(outnorm_grad[None])
        query_grad, key_grad, value_grad, beta_grad, logdecay_grad = pull_mix(mixed_grad)
        raw_grads = pull_prepare(
            (rounded_copy(query_grad), rounded_copy(key_grad), rounded_copy(value_grad))
        )
        beta_raw_grad, decay_raw_grad, grad_log, grad_bias = pull_gates((beta_grad, logdecay_grad))
        leading = (
            raw_grads[0][0],
            raw_grads[1][0],
            raw_grads[2][0],
            gate_raw_grad[0],
            beta_raw_grad[0],
            decay_raw_grad[0],
        )
        leading_back = [piece.astype(jnp.bfloat16) for piece in leading]
        grad_inputs = [against_rows(first_normed, piece) for piece in leading_back]
        first_partial = against_cols(leading_back[0], weights_in[0])
        for position in range(1, 6):
            first_partial = first_partial + against_cols(
                leading_back[position], weights_in[position]
            )
        first_grad = sum_tensor(first_partial)
        grad_mixer = sum_whole(mixer_gain_part, "tensor")
        input_part, grad_first = pull_first(first_grad)
        input_grads.append((middle_grad + input_part).astype(jnp.bfloat16))
        large = grad_inputs + [grad_out, grad_fgate, grad_fup, grad_down]
        small = [
            raw_grads[3],
            raw_grads[4],
            raw_grads[5],
            grad_log,
            grad_bias,
            grad_mixer,
            grad_first,
            grad_second,
        ]
        current = tuple(large) + tuple(small)
        totals = (
            current
            if totals is None
            else tuple((left + right for left, right in zip(totals, current)))
        )
    whole = [sum_dp(totals[k]) if k not in (4, 5) else None for k in range(10)]
    small_shapes = (weights_in[4].shape, weights_in[5].shape) + small_shapes
    flat = jnp.concatenate(
        [piece.reshape(-1) for piece in (totals[4], totals[5]) + tuple(totals[10:])]
    )
    flat = jnp.pad(flat, (0, -flat.shape[0] % 1024)).reshape(-1, 128)
    flat = sum_whole(flat, "dp").reshape(-1)
    pieces = []
    position = 0
    for shape in small_shapes:
        count = 1
        for extent in shape:
            count = count * extent
        pieces.append(flat[position : position + count].reshape(shape))
        position = position + count
    whole[4], whole[5] = pieces[0], pieces[1]
    pieces = pieces[2:]
    return (
        jnp.stack(outputs),
        jnp.stack(input_grads),
        pieces[6],
        whole[0],
        whole[1],
        whole[2],
        whole[3],
        whole[4],
        whole[5],
        pieces[0],
        pieces[1],
        pieces[2],
        pieces[3],
        pieces[4],
        pieces[5],
        whole[6],
        pieces[7],
        whole[7],
        whole[8],
        whole[9],
    )


def solution(mesh):
    in_specs = (
        P("dp", None, None),
        P("dp", None, None),
        P(),
        P(None, "tensor"),
        P(None, "tensor"),
        P(None, "tensor"),
        P(None, "tensor"),
        P(None, "tensor"),
        P(None, "tensor"),
        P(None, "tensor"),
        P(None, "tensor"),
        P(None, "tensor"),
        P("tensor"),
        P("tensor"),
        P(),
        P(None, "tensor"),
        P(),
        P(None, "tensor"),
        P(None, "tensor"),
        P(None, "tensor"),
    )
    out_specs = (
        P("dp", None, None),
        P("dp", None, None),
        P(),
        P(None, "tensor"),
        P(None, "tensor"),
        P(None, "tensor"),
        P(None, "tensor"),
        P(None, "tensor"),
        P(None, "tensor"),
        P(None, "tensor"),
        P(None, "tensor"),
        P(None, "tensor"),
        P("tensor"),
        P("tensor"),
        P(),
        P(None, "tensor"),
        P(),
        P(None, "tensor"),
        P(None, "tensor"),
        P(None, "tensor"),
    )
    return jax.shard_map(body, mesh=mesh, in_specs=in_specs, out_specs=out_specs, check_vma=False)
```

```python
import jax
import jax.numpy as jnp
from jax import lax
from jax.experimental import pallas as pl
from jax.experimental.pallas import tpu as pltpu
from jax.sharding import PartitionSpec as P

DK = 128
DV = 256
EPSILON = 1e-06

CHUNK = 128
WIDE = jnp.float32
HALF = jnp.bfloat16


def dot(left, right, left_axis=1, right_axis=0):
    return lax.dot_general(
        left.astype(HALF),
        right.astype(HALF),
        (((left_axis,), (right_axis,)), ((), ())),
        preferred_element_type=WIDE,
    )


def split(values):
    high = values.astype(HALF)
    return high, (values - high.astype(WIDE)).astype(HALF)


def dot_split(left, right):
    left_high, left_low = split(left)
    right_high, right_low = split(right)
    return dot(left_high, right_high) + (dot(left_high, right_low) + dot(left_low, right_high))


def grid_of(rows, cols):
    row = lax.broadcasted_iota(jnp.int32, (rows, cols), 0)
    col = lax.broadcasted_iota(jnp.int32, (rows, cols), 1)
    return row, col


def sigmoid(values):
    return 1.0 / (1.0 + jnp.exp(-values))


def shift_down(values, steps):
    if steps == 0:
        return values
    row, _ = grid_of(*values.shape)
    return jnp.where(row >= steps, pltpu.roll(values, steps, 0), 0.0)


def shift_up(values, steps):
    if steps == 0:
        return values
    length = values.shape[0]
    row, _ = grid_of(*values.shape)
    return jnp.where(row < length - steps, pltpu.roll(values, length - steps, 0), 0.0)


def filtered(raw, taps):
    width = taps.shape[0]
    total = taps[width - 1 : width] * raw
    for index in range(width - 1):
        total = total + taps[index : index + 1] * shift_down(raw, width - 1 - index)
    return total


def row_norm(values):
    return lax.rsqrt(jnp.sum(values * values, -1, keepdims=True) + EPSILON)


def column(values, index):
    _, lane = grid_of(*values.shape)
    return jnp.sum(jnp.where(lane == index, values, 0.0), -1, keepdims=True)


def chunk_terms(query, key, beta, logdecay):
    row, col = grid_of(CHUNK, CHUNK)
    cum_row = jnp.sum(jnp.where(row <= col, logdecay, 0.0), 0, keepdims=True)
    cum_col = jnp.sum(jnp.where(row == col, cum_row, 0.0), -1, keepdims=True)
    last = cum_row[:, CHUNK - 1 : CHUNK]
    inclusive = row >= col
    decay = jnp.where(inclusive, jnp.exp(jnp.where(inclusive, cum_col - cum_row, 0.0)), 0.0)
    both = dot(jnp.concatenate([query, key], 0), key, 1, 1)
    scores = both[:CHUNK] * decay
    meets = both[CHUNK:]
    lower = jnp.where(row > col, beta * meets * decay, 0.0)
    grow = jnp.exp(cum_col)
    fall = jnp.exp(last - cum_col)
    return decay, scores, meets, lower, grow, fall, jnp.exp(last)


def lower_inverses(lowers):
    row, col = grid_of(CHUNK, CHUNK)
    span = 1
    inverses = None
    while span < CHUNK:
        apart = row ^ col
        mask = (apart >= span) & (apart < 2 * span) & (row > col)
        crosses = [jnp.where(mask, lower, 0.0) for lower in lowers]
        if inverses is None:
            unit = jnp.where(row == col, 1.0, 0.0)
            inverses = [unit - cross for cross in crosses]
        else:
            middles = [INV_DOT(inv, cross) for inv, cross in zip(inverses, crosses)]
            inverses = [inv - INV_DOT(mid, inv) for inv, mid in zip(inverses, middles)]
        span = span * 2
    return inverses


INV_DOT = dot


def open_gates(small_ref, rows_ref, beta_full, decay_full):
    @pl.when(pl.program_id(0) == 0)
    def _():
        raw = small_ref[...]
        beta_full[...] = sigmoid(raw)
        moved = raw + rows_ref[0:1, :]
        soft = jnp.maximum(moved, 0.0) + jnp.log1p(jnp.exp(-jnp.abs(moved)))
        decay_full[...] = -rows_ref[1:2, :] * soft


def forward_kernel(
    query_ref, key_ref, value_ref, gate_ref, small_ref, rows_ref,
    query_taps, key_taps, value_taps, gain_ref,
    out_ref, mixed_ref, fresh_ref, state_ref, inverse_ref,
    beta_full, decay_full,
):
    head = pl.program_id(0)
    heads = pl.num_programs(0)
    length = query_ref.shape[0]
    open_gates(small_ref, rows_ref, beta_full, decay_full)
    beta = column(beta_full[...], head)
    logdecay = column(decay_full[...], heads + head)
    act = filtered(query_ref[...], query_taps[...])
    act = act * sigmoid(act)
    query = (act * row_norm(act) * DK ** (-0.5)).astype(HALF)
    act = filtered(key_ref[...], key_taps[...])
    act = act * sigmoid(act)
    key = (act * row_norm(act)).astype(HALF)
    act = filtered(value_ref[...], value_taps[...])
    value = (act * sigmoid(act)).astype(HALF)
    blocks = length // CHUNK
    terms = []
    for block in range(blocks):
        part = slice(block * CHUNK, (block + 1) * CHUNK)
        terms.append(chunk_terms(query[part], key[part], beta[part], logdecay[part]))
    inverses = lower_inverses([term[3] for term in terms])
    state = jnp.zeros((DK, DV), WIDE)
    gain = gain_ref[...]
    for block in range(blocks):
        part = slice(block * CHUNK, (block + 1) * CHUNK)
        decay, scores, meets, lower, grow, fall, tail = terms[block]
        inverse = inverses[block].astype(HALF)
        inverse_ref[0, block] = inverse
        state_ref[0, block] = state
        both = dot(jnp.concatenate([query[part], key[part]], 0), state)
        write = beta[part] * (value[part].astype(WIDE) - grow * both[CHUNK:])
        fresh = dot(inverse, write)
        fresh_ref[part, :] = fresh
        result = grow * both[:CHUNK] + dot(scores, fresh)
        state = tail * state + dot(fall * key[part].astype(WIDE), fresh, 0, 0)
        mixed_ref[part, :] = result
        gate = gate_ref[part, :]
        scale = lax.rsqrt(jnp.mean(result * result, -1, keepdims=True) + EPSILON)
        out_ref[part, :] = (result * scale * gain * (gate * sigmoid(gate))).astype(HALF)


def filter_back(raw, taps, pre, gate, act_grad, taps_ref):
    width = taps.shape[0]
    edge = act_grad * (gate * (1.0 + pre * (1.0 - gate)))
    total = edge * taps[width - 1 : width]
    sums = [jnp.sum(edge * raw, 0, keepdims=True)]
    for index in range(width - 1):
        moved = shift_up(edge, width - 1 - index)
        total = total + moved * taps[index : index + 1]
        sums.append(jnp.sum(moved * raw, 0, keepdims=True))
    taps_ref[0] = jnp.concatenate(sums[1:] + sums[:1], 0)
    return total


def backward_kernel(
    query_ref, key_ref, value_ref, gate_ref, small_ref, rows_ref,
    query_taps, key_taps, value_taps, gain_ref,
    mixed_ref, fresh_ref, state_ref, inverse_ref, grad_ref,
    query_back, key_back, value_back, gate_back, small_back,
    query_taps_back, key_taps_back, value_taps_back, gain_back,
    beta_full, decay_full, query_grad, key_grad, value_grad,
):
    head = pl.program_id(0)
    heads = pl.num_programs(0)
    length = query_ref.shape[0]
    open_gates(small_ref, rows_ref, beta_full, decay_full)

    @pl.when(head == 0)
    def _():
        small_back[...] = jnp.zeros(small_back.shape, WIDE)
        gain_back[...] = jnp.zeros(gain_back.shape, WIDE)

    beta = column(beta_full[...], head)
    logdecay = column(decay_full[...], heads + head)
    pre_query = filtered(query_ref[...], query_taps[...])
    gate_query = sigmoid(pre_query)
    act_query = pre_query * gate_query
    norm_query = row_norm(act_query)
    query = (act_query * norm_query * DK ** (-0.5)).astype(HALF)
    pre_key = filtered(key_ref[...], key_taps[...])
    gate_key = sigmoid(pre_key)
    act_key = pre_key * gate_key
    norm_key = row_norm(act_key)
    key = (act_key * norm_key).astype(HALF)
    pre_value = filtered(value_ref[...], value_taps[...])
    gate_value = sigmoid(pre_value)
    value = (pre_value * gate_value).astype(HALF)
    gain = gain_ref[...]
    row, col = grid_of(CHUNK, CHUNK)
    blocks = length // CHUNK
    slope = jnp.zeros((DK, DV), WIDE)
    gain_sum = jnp.zeros((1, DV), WIDE)
    beta_grads = [None] * blocks
    decay_grads = [None] * blocks
    for block in range(blocks - 1, -1, -1):
        part = slice(block * CHUNK, (block + 1) * CHUNK)
        mixed = mixed_ref[part, :]
        gate = gate_ref[part, :]
        upper = grad_ref[part, :]
        open_gate = sigmoid(gate)
        silu = gate * open_gate
        scale = lax.rsqrt(jnp.mean(mixed * mixed, -1, keepdims=True) + EPSILON)
        normed = mixed * scale
        gain_sum = gain_sum + jnp.sum(upper * normed * silu, 0, keepdims=True)
        gate_back[part, :] = (
            upper * normed * gain * (open_gate * (1.0 + gate * (1.0 - open_gate)))
        ).astype(HALF)
        pulled = upper * gain * silu
        result_grad = scale * (
            pulled - normed * jnp.mean(pulled * normed, -1, keepdims=True)
        )
        query_part, key_part, beta_part = query[part], key[part], beta[part]
        decay, scores, meets, lower, grow, fall, tail = chunk_terms(
            query_part, key_part, beta_part, logdecay[part]
        )
        inverse = inverse_ref[0, block]
        fresh = fresh_ref[part, :]
        state = state_ref[0, block]
        pair = jnp.concatenate([query_part, key_part], 0)
        both = dot(pair, state)
        rest = value[part].astype(WIDE) - grow * both[CHUNK:]
        faded = fall * key_part.astype(WIDE)
        fresh_grad = dot(scores, result_grad, 0, 0) + dot(faded, slope)
        write_grad = dot(inverse, fresh_grad, 0, 0)
        cross = dot(jnp.concatenate([result_grad, -write_grad], 0), fresh, 1, 1)
        score_grad = jnp.where(row >= col, cross[:CHUNK], 0.0)
        lower_grad = jnp.where(row > col, cross[CHUNK:], 0.0)
        value_part_grad = beta_part * write_grad
        beta_grad = jnp.sum(write_grad * rest, -1, keepdims=True)
        stacked = jnp.concatenate([grow * result_grad, -grow * value_part_grad], 0)
        both_grad = jnp.sum(stacked * both, -1, keepdims=True)
        cum_grad = both_grad[:CHUNK] + both_grad[CHUNK:]
        pair_grad = dot(stacked, state, 1, 1)
        faded_grad = dot(fresh, slope, 1, 1)
        fade = jnp.sum(faded * faded_grad, -1, keepdims=True)
        cum_grad = cum_grad - fade
        last_grad = jnp.sum(fade, 0, keepdims=True) + tail * jnp.sum(
            jnp.sum(state * slope, -1, keepdims=True), 0, keepdims=True
        )
        score_edge = score_grad * decay
        lower_edge = lower_grad * decay
        beta_grad = beta_grad + jnp.sum(lower_edge * meets, -1, keepdims=True)
        lower_edge = lower_edge * beta_part
        spread = score_grad * scores + lower_grad * lower
        cum_grad = cum_grad + jnp.sum(spread, -1, keepdims=True)
        cum_row = (
            jnp.sum(jnp.where(row == col, cum_grad, 0.0), 0, keepdims=True)
            - jnp.sum(spread, 0, keepdims=True)
            + jnp.where(col[:1] == CHUNK - 1, last_grad, 0.0)
        )
        decay_grads[block] = jnp.sum(jnp.where(col >= row, cum_row, 0.0), -1, keepdims=True)
        beta_grads[block] = beta_grad
        edges = jnp.concatenate([score_edge, lower_edge], 0).astype(HALF)
        along = dot(edges, key_part)
        against = dot(edges, pair, 0, 0)
        query_grad[part, :] = (pair_grad[:CHUNK] + along[:CHUNK]).astype(HALF).astype(WIDE)
        key_grad[part, :] = (
            (pair_grad[CHUNK:] + fall * faded_grad + along[CHUNK:] + against)
            .astype(HALF)
            .astype(WIDE)
        )
        value_grad[part, :] = value_part_grad.astype(HALF).astype(WIDE)
        slope = tail * slope + dot(pair, stacked, 0, 0)
    gain_back[0:1, :] = gain_back[0:1, :] + gain_sum

    back = query_grad[...]
    inner = jnp.sum(act_query * back, -1, keepdims=True)
    act_grad = DK ** (-0.5) * (norm_query * (back - act_query * (norm_query * norm_query * inner)))
    query_back[...] = filter_back(
        query_ref[...], query_taps[...], pre_query, gate_query, act_grad, query_taps_back
    ).astype(HALF)
    back = key_grad[...]
    inner = jnp.sum(act_key * back, -1, keepdims=True)
    act_grad = norm_key * (back - act_key * (norm_key * norm_key * inner))
    key_back[...] = filter_back(
        key_ref[...], key_taps[...], pre_key, gate_key, act_grad, key_taps_back
    ).astype(HALF)
    value_back[...] = filter_back(
        value_ref[...], value_taps[...], pre_value, gate_value, value_grad[...], value_taps_back
    ).astype(HALF)
    beta_grad = jnp.concatenate(beta_grads, 0)
    decay_grad = jnp.concatenate(decay_grads, 0)
    beta_raw_grad = beta_grad * beta * (1.0 - beta)
    _, lane = grid_of(length, small_back.shape[1])
    moved = small_ref[...] + rows_ref[0:1, :]
    slopes = jnp.where(lane < 2 * heads, -rows_ref[1:2, :] * sigmoid(moved), 0.0)
    update = jnp.where(lane == head, beta_raw_grad, 0.0)
    update = update + jnp.where(lane == heads + head, decay_grad * slopes, 0.0)
    update = update + jnp.where(lane == 2 * heads + head, decay_grad * logdecay, 0.0)
    small_back[...] = small_back[...] + update


def whole_spec(shape):
    return pl.BlockSpec(shape, lambda head: (0,) * len(shape))


def head_spec(rows, width):
    return pl.BlockSpec((rows, width), lambda head: (0, head))


def stack_spec(*shape):
    return pl.BlockSpec((1,) + shape, lambda head: (head,) + (0,) * len(shape))


def mixer_specs(length, width, gain_width):
    return [
        head_spec(length, DK), head_spec(length, DK), head_spec(length, DV), head_spec(length, DV),
        whole_spec((length, 128)), whole_spec((8, 128)),
        head_spec(width, DK), head_spec(width, DK), head_spec(width, DV),
        whole_spec((1, gain_width)),
    ]


def mixer_forward(query, key, value, gate, small, rows, query_taps, key_taps, value_taps, gain):
    length = query.shape[0]
    heads = query.shape[1] // DK
    width = query_taps.shape[0]
    blocks = length // CHUNK
    wide = value.shape[1]
    shape = jax.ShapeDtypeStruct
    return pl.pallas_call(
        forward_kernel,
        grid=(heads,),
        in_specs=mixer_specs(length, width, DV),
        out_specs=[
            head_spec(length, DV), head_spec(length, DV), head_spec(length, DV),
            stack_spec(blocks, DK, DV), stack_spec(blocks, CHUNK, CHUNK),
        ],
        out_shape=[
            shape((length, wide), HALF), shape((length, wide), WIDE), shape((length, wide), WIDE),
            shape((heads, blocks, DK, DV), WIDE), shape((heads, blocks, CHUNK, CHUNK), HALF),
        ],
        scratch_shapes=[pltpu.VMEM((length, 128), WIDE), pltpu.VMEM((length, 128), WIDE)],
        name="mixer_forward",
    )(query, key, value, gate, small, rows, query_taps, key_taps, value_taps, gain[None])


def mixer_backward(operands, kept, grad):
    query, key, value, gate, small, rows, query_taps, key_taps, value_taps, gain = operands
    length = query.shape[0]
    heads = query.shape[1] // DK
    width = query_taps.shape[0]
    blocks = length // CHUNK
    narrow, wide = query.shape[1], value.shape[1]
    shape = jax.ShapeDtypeStruct
    return pl.pallas_call(
        backward_kernel,
        grid=(heads,),
        in_specs=mixer_specs(length, width, DV) + [
            head_spec(length, DV), head_spec(length, DV),
            stack_spec(blocks, DK, DV), stack_spec(blocks, CHUNK, CHUNK),
            head_spec(length, DV),
        ],
        out_specs=[
            head_spec(length, DK), head_spec(length, DK), head_spec(length, DV),
            head_spec(length, DV), whole_spec((length, 128)),
            stack_spec(width, DK), stack_spec(width, DK), stack_spec(width, DV),
            whole_spec((8, DV)),
        ],
        out_shape=[
            shape((length, narrow), HALF), shape((length, narrow), HALF),
            shape((length, wide), HALF), shape((length, wide), HALF),
            shape((length, 128), WIDE),
            shape((heads, width, DK), WIDE), shape((heads, width, DK), WIDE),
            shape((heads, width, DV), WIDE), shape((8, DV), WIDE),
        ],
        scratch_shapes=[
            pltpu.VMEM((length, 128), WIDE), pltpu.VMEM((length, 128), WIDE),
            pltpu.VMEM((length, DK), WIDE), pltpu.VMEM((length, DK), WIDE),
            pltpu.VMEM((length, DV), WIDE),
        ],
        name="mixer_backward",
    )(query, key, value, gate, small, rows, query_taps, key_taps, value_taps, gain[None], *kept, grad)


def root_norm(values, gain):
    return values * lax.rsqrt(jnp.mean(values * values, -1, keepdims=True) + EPSILON) * gain


def swiglu(gate, upward):
    return jax.nn.silu(gate) * upward


def matmul(left, right):
    return jnp.dot(left, right, preferred_element_type=jnp.float32)


def against_rows(left, right):
    return lax.dot_general(
        left, right, (((0,), (0,)), ((), ())), preferred_element_type=jnp.float32
    )


def against_cols(left, right):
    return lax.dot_general(
        left, right, (((1,), (1,)), ((), ())), preferred_element_type=jnp.float32
    )


def swap_pairs(size, bit):
    return [(index, index ^ (1 << bit)) for index in range(size)]


def bits_of(size):
    return list(range(size.bit_length() - 1))


def halve(values, axis, bit):
    size = lax.axis_size(axis)
    upper = (lax.axis_index(axis) >> bit) & 1
    half = values.shape[0] // 2
    kept = lax.dynamic_slice_in_dim(values, upper * half, half, 0)
    given = lax.dynamic_slice_in_dim(values, (1 - upper) * half, half, 0)
    return kept + lax.ppermute(given, axis, swap_pairs(size, bit))


def double(values, axis, bit):
    size = lax.axis_size(axis)
    upper = (lax.axis_index(axis) >> bit) & 1
    other = lax.ppermute(values, axis, swap_pairs(size, bit))
    half = values.shape[0]
    whole = jnp.zeros((2 * half,) + values.shape[1:], values.dtype)
    whole = lax.dynamic_update_slice_in_dim(whole, values, upper * half, 0)
    return lax.dynamic_update_slice_in_dim(whole, other, (1 - upper) * half, 0)


def sum_by_halves(values, axis, order):
    for bit in order:
        values = halve(values, axis, bit)
    for bit in reversed(order):
        values = double(values, axis, bit)
    return values


def sum_whole(values, axis):
    size = lax.axis_size(axis)
    for bit in bits_of(size):
        values = values + lax.ppermute(values, axis, swap_pairs(size, bit))
    return values


def sum_tensor(values):
    size = lax.axis_size("tensor")
    values = halve(values, "tensor", 0)
    for bit in bits_of(size)[1:]:
        values = values + lax.ppermute(values, "tensor", swap_pairs(size, bit))
    return double(values, "tensor", 0)


def sum_dp(values, crossed):
    order = bits_of(lax.axis_size("dp"))
    if crossed:
        order = [1, 0] + order[2:]
    return sum_by_halves(values, "dp", order)


def join_heads(stack):
    return jnp.swapaxes(stack, 0, 1).reshape(stack.shape[1], -1)


def body(
    tokens,
    out_grad,
    first_gain,
    query_weight,
    key_weight,
    value_weight,
    gate_weight,
    beta_weight,
    decay_weight,
    query_filter,
    key_filter,
    value_filter,
    decay_log,
    decay_bias,
    mixer_gain,
    out_weight,
    second_gain,
    ffn_gate_weight,
    ffn_up_weight,
    ffn_down_weight,
):
    heads = query_weight.shape[1] // DK
    count = tokens.shape[0]
    filters = tuple(
        taps.astype(jnp.float32) for taps in (query_filter, key_filter, value_filter)
    )
    small_weight = jnp.concatenate([beta_weight, decay_weight], 1)
    small_weight = jnp.pad(small_weight, ((0, 0), (0, 128 - 2 * heads)))
    rows = jnp.stack([decay_bias, jnp.exp(decay_log)])
    rows = jnp.pad(rows, ((0, 6), (heads, 128 - 2 * heads)))

    first_normed, pull_first, operands, kept, mixer_out, inputs = [], [], [], [], [], []
    for index in range(count):
        inputs.append(tokens[index].astype(jnp.float32))
        first_float, pull = jax.vjp(root_norm, inputs[index], first_gain)
        pull_first.append(pull)
        normed = first_float.astype(jnp.bfloat16)
        first_normed.append(normed)
        raws = [
            matmul(normed, weight)
            for weight in (query_weight, key_weight, value_weight, gate_weight, small_weight)
        ]
        operands.append((*raws, rows, *filters, mixer_gain))
        out, *saved = mixer_forward(*operands[index])
        mixer_out.append(out)
        kept.append(saved)
    middle, outputs, hidden, second_normed = [], [], [], []
    gate_back, up_back, middle_grad, mixer_back, grad_second = [], [], [], [], []
    for index in range(count):
        middle.append(inputs[index] + sum_tensor(against_cols(mixer_out[index], out_weight)))
        second_float, pull_second = jax.vjp(root_norm, middle[index], second_gain)
        second_normed.append(second_float.astype(jnp.bfloat16))
        ffn_gate = matmul(second_normed[index], ffn_gate_weight)
        ffn_up = matmul(second_normed[index], ffn_up_weight)
        hidden_float, pull_swiglu = jax.vjp(swiglu, ffn_gate, ffn_up)
        hidden.append(hidden_float.astype(jnp.bfloat16))
        hidden_grad = matmul(out_grad[index], ffn_down_weight)
        gate_grad, up_grad = pull_swiglu(hidden_grad)
        gate_back.append(gate_grad.astype(jnp.bfloat16))
        up_back.append(up_grad.astype(jnp.bfloat16))
        second_partial = against_cols(gate_back[index], ffn_gate_weight) + against_cols(
            up_back[index], ffn_up_weight
        )
        second_grad = sum_tensor(second_partial)
        middle_part, part = pull_second(second_grad)
        grad_second.append(part)
        middle_grad.append(out_grad[index].astype(jnp.float32) + middle_part)
        mixer_back.append(middle_grad[index].astype(jnp.bfloat16))
    for index in range(count):
        ffn_sum = sum_tensor(against_cols(hidden[index], ffn_down_weight))
        outputs.append((middle[index] + ffn_sum).astype(jnp.bfloat16))

    def joined(pieces):
        return jnp.concatenate(pieces, 0)

    ffn_back = out_grad.reshape(-1, out_grad.shape[-1])
    normed = joined(second_normed)
    grad_down = sum_dp(against_rows(ffn_back, joined(hidden)), False)
    grad_fgate = sum_dp(against_rows(normed, joined(gate_back)), True)
    grad_fup = sum_dp(against_rows(normed, joined(up_back)), False)
    grad_out = sum_dp(against_rows(joined(mixer_back), joined(mixer_out)), False)

    backs, taps_back = [], []
    gain_back, input_grads, grad_first = [], [], []
    for index in range(count):
        outnorm_grad = matmul(mixer_back[index], out_weight)
        result = mixer_backward(operands[index], kept[index], outnorm_grad)
        query_back, key_back, value_back, gate_mix, small_grad, *taps, gain_part = result
        backs.append((query_back, key_back, value_back, gate_mix, small_grad))
        taps_back.append([join_heads(piece) for piece in taps])
        gain_back.append(gain_part[0])
    weights = (query_weight, key_weight, value_weight, gate_weight, small_weight)
    normed = joined(first_normed)
    pieces = [joined([back[place] for back in backs]) for place in range(5)]
    small_sums = jnp.sum(pieces[4], 0)
    pieces[4] = pieces[4].astype(jnp.bfloat16)
    grads = [against_rows(normed, piece) for piece in pieces]
    grad_gate = sum_dp(grads[3], True)
    grad_value = sum_dp(grads[2], False)
    grad_key = sum_dp(grads[1], False)
    grad_query = sum_dp(grads[0], True)
    for index in range(count):
        first_partial = against_cols(backs[index][4].astype(jnp.bfloat16), small_weight)
        for place in range(4):
            first_partial = first_partial + against_cols(backs[index][place], weights[place])
        input_part, part = pull_first[index](sum_tensor(first_partial))
        grad_first.append(part)
        input_grads.append((middle_grad[index] + input_part).astype(jnp.bfloat16))

    def total(parts):
        whole = parts[0]
        for part in parts[1:]:
            whole = whole + part
        return whole

    small = [
        grads[4][:, :heads],
        grads[4][:, heads : 2 * heads],
        total([taps[0] for taps in taps_back]),
        total([taps[1] for taps in taps_back]),
        total([taps[2] for taps in taps_back]),
        small_sums[2 * heads : 3 * heads],
        small_sums[heads : 2 * heads],
        sum_whole(total(gain_back), "tensor"),
        total(grad_first),
        total(grad_second),
    ]
    flat = jnp.concatenate([piece.reshape(-1) for piece in small])
    flat = jnp.pad(flat, (0, -flat.shape[0] % 1024)).reshape(-1, 128)
    flat = sum_whole(flat, "dp").reshape(-1)
    parts = []
    position = 0
    for piece in small:
        parts.append(flat[position : position + piece.size].reshape(piece.shape))
        position = position + piece.size
    return (
        jnp.stack(outputs),
        jnp.stack(input_grads),
        parts[8],
        grad_query,
        grad_key,
        grad_value,
        grad_gate,
        parts[0],
        parts[1],
        parts[2],
        parts[3],
        parts[4],
        parts[5],
        parts[6],
        parts[7],
        grad_out,
        parts[9],
        grad_fgate,
        grad_fup,
        grad_down,
    )


def solution(mesh):
    in_specs = (
        P("dp", None, None),
        P("dp", None, None),
        P(),
        P(None, "tensor"),
        P(None, "tensor"),
        P(None, "tensor"),
        P(None, "tensor"),
        P(None, "tensor"),
        P(None, "tensor"),
        P(None, "tensor"),
        P(None, "tensor"),
        P(None, "tensor"),
        P("tensor"),
        P("tensor"),
        P(),
        P(None, "tensor"),
        P(),
        P(None, "tensor"),
        P(None, "tensor"),
        P(None, "tensor"),
    )
    out_specs = (
        P("dp", None, None),
        P("dp", None, None),
        P(),
        P(None, "tensor"),
        P(None, "tensor"),
        P(None, "tensor"),
        P(None, "tensor"),
        P(None, "tensor"),
        P(None, "tensor"),
        P(None, "tensor"),
        P(None, "tensor"),
        P(None, "tensor"),
        P("tensor"),
        P("tensor"),
        P(),
        P(None, "tensor"),
        P(),
        P(None, "tensor"),
        P(None, "tensor"),
        P(None, "tensor"),
    )
    return jax.shard_map(body, mesh=mesh, in_specs=in_specs, out_specs=out_specs, check_vma=False)
```

```python
import jax
import jax.numpy as jnp
from jax import lax
from jax.experimental import pallas as pl
from jax.experimental.pallas import tpu as pltpu
from jax.sharding import PartitionSpec as P


DK = 128
DV = 256
EPSILON = 1e-06

CHUNK = 128
WIDE = jnp.float32
HALF = jnp.bfloat16


def dot(left, right, left_axis=1, right_axis=0):
    return lax.dot_general(
        left.astype(HALF),
        right.astype(HALF),
        (((left_axis,), (right_axis,)), ((), ())),
        preferred_element_type=WIDE,
    )


def grid_of(rows, cols):
    row = lax.broadcasted_iota(jnp.int32, (rows, cols), 0)
    col = lax.broadcasted_iota(jnp.int32, (rows, cols), 1)
    return row, col


def sigmoid(values):
    return 1.0 / (1.0 + jnp.exp(-values))


def shift_down(values, steps):
    if steps == 0:
        return values
    row, _ = grid_of(*values.shape)
    return jnp.where(row >= steps, pltpu.roll(values, steps, 0), 0.0)


def shift_up(values, steps):
    if steps == 0:
        return values
    length = values.shape[0]
    row, _ = grid_of(*values.shape)
    return jnp.where(row < length - steps, pltpu.roll(values, length - steps, 0), 0.0)


def filtered(raw, taps):
    width = taps.shape[0]
    total = taps[width - 1 : width] * raw
    for index in range(width - 1):
        total = total + taps[index : index + 1] * shift_down(raw, width - 1 - index)
    return total


def row_norm(values):
    return lax.rsqrt(jnp.sum(values * values, -1, keepdims=True) + EPSILON)


def column(values, index):
    _, lane = grid_of(*values.shape)
    return jnp.sum(jnp.where(lane == index, values, 0.0), -1, keepdims=True)


def chunk_terms(query, key, beta, logdecay):
    row, col = grid_of(CHUNK, CHUNK)
    cum_row = jnp.sum(jnp.where(row <= col, logdecay, 0.0), 0, keepdims=True)
    cum_col = jnp.sum(jnp.where(row == col, cum_row, 0.0), -1, keepdims=True)
    last = cum_row[:, CHUNK - 1 : CHUNK]
    inclusive = row >= col
    decay = jnp.where(inclusive, jnp.exp(jnp.where(inclusive, cum_col - cum_row, 0.0)), 0.0)
    both = dot(jnp.concatenate([query, key], 0), key, 1, 1)
    scores = both[:CHUNK] * decay
    meets = both[CHUNK:]
    lower = jnp.where(row > col, beta * meets * decay, 0.0)
    grow = jnp.exp(cum_col)
    fall = jnp.exp(last - cum_col)
    return decay, scores, meets, lower, grow, fall, jnp.exp(last)


def lower_inverses(lowers):
    row, col = grid_of(CHUNK, CHUNK)
    span = 1
    inverses = None
    while span < CHUNK:
        apart = row ^ col
        mask = (apart >= span) & (apart < 2 * span) & (row > col)
        crosses = [jnp.where(mask, lower, 0.0) for lower in lowers]
        if inverses is None:
            unit = jnp.where(row == col, 1.0, 0.0)
            inverses = [unit - cross for cross in crosses]
        else:
            middles = [INV_DOT(inv, cross) for inv, cross in zip(inverses, crosses)]
            inverses = [inv - INV_DOT(mid, inv) for inv, mid in zip(inverses, middles)]
        span = span * 2
    return inverses


INV_DOT = dot


def open_gates(small_ref, rows_ref, beta_full, decay_full):
    @pl.when(pl.program_id(0) == 0)
    def _():
        raw = small_ref[...]
        beta_full[...] = sigmoid(raw)
        moved = raw + rows_ref[0:1, :]
        soft = jnp.maximum(moved, 0.0) + jnp.log1p(jnp.exp(-jnp.abs(moved)))
        decay_full[...] = -rows_ref[1:2, :] * soft


def forward_kernel(
    query_ref, key_ref, value_ref, gate_ref, small_ref, rows_ref,
    query_taps, key_taps, value_taps, gain_ref,
    out_ref, mixed_ref, fresh_ref, state_ref, inverse_ref,
    beta_full, decay_full,
):
    head = pl.program_id(0)
    heads = pl.num_programs(0)
    length = query_ref.shape[0]
    open_gates(small_ref, rows_ref, beta_full, decay_full)
    beta = column(beta_full[...], head)
    logdecay = column(decay_full[...], heads + head)
    act = filtered(query_ref[...], query_taps[...])
    act = act * sigmoid(act)
    query = (act * row_norm(act) * DK ** (-0.5)).astype(HALF)
    act = filtered(key_ref[...], key_taps[...])
    act = act * sigmoid(act)
    key = (act * row_norm(act)).astype(HALF)
    act = filtered(value_ref[...], value_taps[...])
    value = (act * sigmoid(act)).astype(HALF)
    blocks = length // CHUNK
    terms = []
    for block in range(blocks):
        part = slice(block * CHUNK, (block + 1) * CHUNK)
        terms.append(chunk_terms(query[part], key[part], beta[part], logdecay[part]))
    inverses = lower_inverses([term[3] for term in terms])
    state = jnp.zeros((DK, DV), WIDE)
    gain = gain_ref[...]
    for block in range(blocks):
        part = slice(block * CHUNK, (block + 1) * CHUNK)
        _, scores, _, _, grow, fall, tail = terms[block]
        inverse = inverses[block].astype(HALF)
        inverse_ref[0, block] = inverse
        state_ref[0, block] = state
        both = dot(jnp.concatenate([query[part], key[part]], 0), state)
        write = beta[part] * (value[part].astype(WIDE) - grow * both[CHUNK:])
        fresh = dot(inverse, write)
        fresh_ref[part, :] = fresh
        result = grow * both[:CHUNK] + dot(scores, fresh)
        state = tail * state + dot(fall * key[part].astype(WIDE), fresh, 0, 0)
        mixed_ref[part, :] = result
        gate = gate_ref[part, :]
        scale = lax.rsqrt(jnp.mean(result * result, -1, keepdims=True) + EPSILON)
        out_ref[part, :] = (result * scale * gain * (gate * sigmoid(gate))).astype(HALF)


def filter_back(raw, taps, pre, gate, act_grad, taps_ref):
    width = taps.shape[0]
    edge = act_grad * (gate * (1.0 + pre * (1.0 - gate)))
    total = edge * taps[width - 1 : width]
    sums = [jnp.sum(edge * raw, 0, keepdims=True)]
    for index in range(width - 1):
        moved = shift_up(edge, width - 1 - index)
        total = total + moved * taps[index : index + 1]
        sums.append(jnp.sum(moved * raw, 0, keepdims=True))
    taps_ref[0] = jnp.concatenate(sums[1:] + sums[:1], 0)
    return total


def backward_kernel(
    query_ref, key_ref, value_ref, gate_ref, small_ref, rows_ref,
    query_taps, key_taps, value_taps, gain_ref,
    mixed_ref, fresh_ref, state_ref, inverse_ref, grad_ref,
    query_back, key_back, value_back, gate_back, small_back,
    query_taps_back, key_taps_back, value_taps_back, gain_back,
    beta_full, decay_full, query_grad, key_grad, value_grad,
):
    head = pl.program_id(0)
    heads = pl.num_programs(0)
    length = query_ref.shape[0]
    open_gates(small_ref, rows_ref, beta_full, decay_full)

    @pl.when(head == 0)
    def _():
        small_back[...] = jnp.zeros(small_back.shape, WIDE)
        gain_back[...] = jnp.zeros(gain_back.shape, WIDE)

    beta = column(beta_full[...], head)
    logdecay = column(decay_full[...], heads + head)
    pre_query = filtered(query_ref[...], query_taps[...])
    gate_query = sigmoid(pre_query)
    act_query = pre_query * gate_query
    norm_query = row_norm(act_query)
    query = (act_query * norm_query * DK ** (-0.5)).astype(HALF)
    pre_key = filtered(key_ref[...], key_taps[...])
    gate_key = sigmoid(pre_key)
    act_key = pre_key * gate_key
    norm_key = row_norm(act_key)
    key = (act_key * norm_key).astype(HALF)
    pre_value = filtered(value_ref[...], value_taps[...])
    gate_value = sigmoid(pre_value)
    value = (pre_value * gate_value).astype(HALF)
    gain = gain_ref[...]
    row, col = grid_of(CHUNK, CHUNK)
    blocks = length // CHUNK
    slope = jnp.zeros((DK, DV), WIDE)
    gain_sum = jnp.zeros((1, DV), WIDE)
    beta_grads = [None] * blocks
    decay_grads = [None] * blocks
    for block in range(blocks - 1, -1, -1):
        part = slice(block * CHUNK, (block + 1) * CHUNK)
        mixed = mixed_ref[part, :]
        gate = gate_ref[part, :]
        upper = grad_ref[part, :]
        open_gate = sigmoid(gate)
        silu = gate * open_gate
        scale = lax.rsqrt(jnp.mean(mixed * mixed, -1, keepdims=True) + EPSILON)
        normed = mixed * scale
        gain_sum = gain_sum + jnp.sum(upper * normed * silu, 0, keepdims=True)
        gate_back[part, :] = (
            upper * normed * gain * (open_gate * (1.0 + gate * (1.0 - open_gate)))
        ).astype(HALF)
        pulled = upper * gain * silu
        result_grad = scale * (
            pulled - normed * jnp.mean(pulled * normed, -1, keepdims=True)
        )
        query_part, key_part, beta_part = query[part], key[part], beta[part]
        decay, scores, meets, lower, grow, fall, tail = chunk_terms(
            query_part, key_part, beta_part, logdecay[part]
        )
        inverse = inverse_ref[0, block]
        fresh = fresh_ref[part, :]
        state = state_ref[0, block]
        pair = jnp.concatenate([query_part, key_part], 0)
        both = dot(pair, state)
        rest = value[part].astype(WIDE) - grow * both[CHUNK:]
        faded = fall * key_part.astype(WIDE)
        fresh_grad = dot(scores, result_grad, 0, 0) + dot(faded, slope)
        write_grad = dot(inverse, fresh_grad, 0, 0)
        cross = dot(jnp.concatenate([result_grad, -write_grad], 0), fresh, 1, 1)
        score_grad = jnp.where(row >= col, cross[:CHUNK], 0.0)
        lower_grad = jnp.where(row > col, cross[CHUNK:], 0.0)
        value_part_grad = beta_part * write_grad
        beta_grad = jnp.sum(write_grad * rest, -1, keepdims=True)
        stacked = jnp.concatenate([grow * result_grad, -grow * value_part_grad], 0)
        both_grad = jnp.sum(stacked * both, -1, keepdims=True)
        cum_grad = both_grad[:CHUNK] + both_grad[CHUNK:]
        pair_grad = dot(stacked, state, 1, 1)
        faded_grad = dot(fresh, slope, 1, 1)
        fade = jnp.sum(faded * faded_grad, -1, keepdims=True)
        cum_grad = cum_grad - fade
        last_grad = jnp.sum(fade, 0, keepdims=True) + tail * jnp.sum(
            jnp.sum(state * slope, -1, keepdims=True), 0, keepdims=True
        )
        score_edge = score_grad * decay
        lower_edge = lower_grad * decay
        beta_grad = beta_grad + jnp.sum(lower_edge * meets, -1, keepdims=True)
        lower_edge = lower_edge * beta_part
        spread = score_grad * scores + lower_grad * lower
        cum_grad = cum_grad + jnp.sum(spread, -1, keepdims=True)
        cum_row = (
            jnp.sum(jnp.where(row == col, cum_grad, 0.0), 0, keepdims=True)
            - jnp.sum(spread, 0, keepdims=True)
            + jnp.where(col[:1] == CHUNK - 1, last_grad, 0.0)
        )
        decay_grads[block] = jnp.sum(jnp.where(col >= row, cum_row, 0.0), -1, keepdims=True)
        beta_grads[block] = beta_grad
        edges = jnp.concatenate([score_edge, lower_edge], 0).astype(HALF)
        along = dot(edges, key_part)
        against = dot(edges, pair, 0, 0)
        query_grad[part, :] = (pair_grad[:CHUNK] + along[:CHUNK]).astype(HALF).astype(WIDE)
        key_grad[part, :] = (
            (pair_grad[CHUNK:] + fall * faded_grad + along[CHUNK:] + against)
            .astype(HALF)
            .astype(WIDE)
        )
        value_grad[part, :] = value_part_grad.astype(HALF).astype(WIDE)
        slope = tail * slope + dot(pair, stacked, 0, 0)
    gain_back[0:1, :] = gain_back[0:1, :] + gain_sum

    back = query_grad[...]
    inner = jnp.sum(act_query * back, -1, keepdims=True)
    act_grad = DK ** (-0.5) * (norm_query * (back - act_query * (norm_query * norm_query * inner)))
    query_back[...] = filter_back(
        query_ref[...], query_taps[...], pre_query, gate_query, act_grad, query_taps_back
    ).astype(HALF)
    back = key_grad[...]
    inner = jnp.sum(act_key * back, -1, keepdims=True)
    act_grad = norm_key * (back - act_key * (norm_key * norm_key * inner))
    key_back[...] = filter_back(
        key_ref[...], key_taps[...], pre_key, gate_key, act_grad, key_taps_back
    ).astype(HALF)
    value_back[...] = filter_back(
        value_ref[...], value_taps[...], pre_value, gate_value, value_grad[...], value_taps_back
    ).astype(HALF)
    beta_grad = jnp.concatenate(beta_grads, 0)
    decay_grad = jnp.concatenate(decay_grads, 0)
    beta_raw_grad = beta_grad * beta * (1.0 - beta)
    _, lane = grid_of(length, small_back.shape[1])
    moved = small_ref[...] + rows_ref[0:1, :]
    slopes = jnp.where(lane < 2 * heads, -rows_ref[1:2, :] * sigmoid(moved), 0.0)
    update = jnp.where(lane == head, beta_raw_grad, 0.0)
    update = update + jnp.where(lane == heads + head, decay_grad * slopes, 0.0)
    update = update + jnp.where(lane == 2 * heads + head, decay_grad * logdecay, 0.0)
    small_back[...] = small_back[...] + update


def cost(micros):
    return pl.CostEstimate(flops=micros * 10**9, bytes_accessed=micros * 3 * 10**6, transcendentals=0)


def whole_spec(shape):
    return pl.BlockSpec(shape, lambda head: (0,) * len(shape))


def head_spec(rows, width):
    return pl.BlockSpec((rows, width), lambda head: (0, head))


def stack_spec(*shape):
    return pl.BlockSpec((1,) + shape, lambda head: (head,) + (0,) * len(shape))


def mixer_specs(length, width, gain_width):
    return [
        head_spec(length, DK), head_spec(length, DK), head_spec(length, DV), head_spec(length, DV),
        whole_spec((length, 128)), whole_spec((8, 128)),
        head_spec(width, DK), head_spec(width, DK), head_spec(width, DV),
        whole_spec((1, gain_width)),
    ]


def mixer_forward(query, key, value, gate, small, rows, query_taps, key_taps, value_taps, gain):
    length = query.shape[0]
    heads = query.shape[1] // DK
    width = query_taps.shape[0]
    blocks = length // CHUNK
    wide = value.shape[1]
    shape = jax.ShapeDtypeStruct
    return pl.pallas_call(
        forward_kernel,
        grid=(heads,),
        in_specs=mixer_specs(length, width, DV),
        out_specs=[
            head_spec(length, DV), head_spec(length, DV), head_spec(length, DV),
            stack_spec(blocks, DK, DV), stack_spec(blocks, CHUNK, CHUNK),
        ],
        out_shape=[
            shape((length, wide), HALF), shape((length, wide), WIDE), shape((length, wide), WIDE),
            shape((heads, blocks, DK, DV), WIDE), shape((heads, blocks, CHUNK, CHUNK), HALF),
        ],
        scratch_shapes=[pltpu.VMEM((length, 128), WIDE), pltpu.VMEM((length, 128), WIDE)],
        cost_estimate=cost(20),
        name="mixer_forward",
    )(query, key, value, gate, small, rows, query_taps, key_taps, value_taps, gain[None])


def mixer_backward(operands, kept, grad):
    query, key, value, gate, small, rows, query_taps, key_taps, value_taps, gain = operands
    length = query.shape[0]
    heads = query.shape[1] // DK
    width = query_taps.shape[0]
    blocks = length // CHUNK
    narrow, wide = query.shape[1], value.shape[1]
    shape = jax.ShapeDtypeStruct
    return pl.pallas_call(
        backward_kernel,
        grid=(heads,),
        in_specs=mixer_specs(length, width, DV) + [
            head_spec(length, DV), head_spec(length, DV),
            stack_spec(blocks, DK, DV), stack_spec(blocks, CHUNK, CHUNK),
            head_spec(length, DV),
        ],
        out_specs=[
            head_spec(length, DK), head_spec(length, DK), head_spec(length, DV),
            head_spec(length, DV), whole_spec((length, 128)),
            stack_spec(width, DK), stack_spec(width, DK), stack_spec(width, DV),
            whole_spec((8, DV)),
        ],
        out_shape=[
            shape((length, narrow), HALF), shape((length, narrow), HALF),
            shape((length, wide), HALF), shape((length, wide), HALF),
            shape((length, 128), WIDE),
            shape((heads, width, DK), WIDE), shape((heads, width, DK), WIDE),
            shape((heads, width, DV), WIDE), shape((8, DV), WIDE),
        ],
        scratch_shapes=[
            pltpu.VMEM((length, 128), WIDE), pltpu.VMEM((length, 128), WIDE),
            pltpu.VMEM((length, DK), WIDE), pltpu.VMEM((length, DK), WIDE),
            pltpu.VMEM((length, DV), WIDE),
        ],
        cost_estimate=cost(24),
        name="mixer_backward",
    )(query, key, value, gate, small, rows, query_taps, key_taps, value_taps, gain[None], *kept, grad)


def root_norm(values, gain):
    return values * lax.rsqrt(jnp.mean(values * values, -1, keepdims=True) + EPSILON) * gain


def swiglu(gate, upward):
    return jax.nn.silu(gate) * upward


def matmul(left, right):
    return jnp.dot(left, right, preferred_element_type=jnp.float32)


def against_rows(left, right):
    return lax.dot_general(
        left, right, (((0,), (0,)), ((), ())), preferred_element_type=jnp.float32
    )


def against_cols(left, right):
    return lax.dot_general(
        left, right, (((1,), (1,)), ((), ())), preferred_element_type=jnp.float32
    )


def after(value, *marks):
    return lax.optimization_barrier((value,) + marks)[0]


def swap_pairs(size, bit):
    return [(index, index ^ (1 << bit)) for index in range(size)]


def bits_of(size):
    return list(range(size.bit_length() - 1))


def halve(values, axis, bit):
    size = lax.axis_size(axis)
    upper = (lax.axis_index(axis) >> bit) & 1
    half = values.shape[0] // 2
    kept = lax.dynamic_slice_in_dim(values, upper * half, half, 0)
    given = lax.dynamic_slice_in_dim(values, (1 - upper) * half, half, 0)
    return kept + lax.ppermute(given, axis, swap_pairs(size, bit))


def double(values, axis, bit, base):
    size = lax.axis_size(axis)
    upper = (lax.axis_index(axis) >> bit) & 1
    other = lax.ppermute(values, axis, swap_pairs(size, bit))
    half = values.shape[0]
    whole = lax.dynamic_update_slice_in_dim(base, values, upper * half, 0)
    return lax.dynamic_update_slice_in_dim(whole, other, (1 - upper) * half, 0)


def sum_by_halves(values, axis, order):
    bases = []
    for bit in order:
        bases.append(values)
        values = halve(values, axis, bit)
    for bit in reversed(order):
        values = double(values, axis, bit, bases.pop())
    return values


def sum_whole(values, axis):
    size = lax.axis_size(axis)
    for bit in bits_of(size):
        values = values + lax.ppermute(values, axis, swap_pairs(size, bit))
    return values


def open_tensor(values):
    return values, halve(values, "tensor", 0)


def close_tensor(opened):
    base, values = opened
    size = lax.axis_size("tensor")
    for bit in bits_of(size)[1:]:
        values = values + lax.ppermute(values, "tensor", swap_pairs(size, bit))
    return double(values, "tensor", 0, base)


def sum_tensor(values):
    return close_tensor(open_tensor(values))


def sum_dp(values, crossed):
    order = bits_of(lax.axis_size("dp"))
    if crossed:
        order = [1, 0] + order[2:]
    return sum_by_halves(values, "dp", order)


def ring_of(size):
    return list(range(0, size, 2)) + list(range(size - 1, 0, -2))


def sum_ring(values, cuts=()):
    size = lax.axis_size("dp")
    edges = [0, *cuts, values.shape[1]]
    if size > 8:
        whole = sum_dp(values, False)
        return [whole[:, low:high] for low, high in zip(edges, edges[1:])]
    ring = ring_of(size)
    places = [ring.index(device) for device in range(size)]
    place = jnp.array(places, jnp.int32)[lax.axis_index("dp")]
    ahead = [(ring[step], ring[(step + 1) % size]) for step in range(size)]
    behind = [(target, source) for source, target in ahead]
    rows = values.shape[0] // size
    half = (rows + 15) // 16 * 8
    extents = (half, rows - half)

    def start_of(block, side):
        return ((place + block) % size) * rows + side * half

    def part(block, side):
        return lax.dynamic_slice_in_dim(values, start_of(block, side), extents[side], 0)

    def pass_on(sends):
        first = lax.ppermute(sends[0], "dp", ahead)
        second = lax.ppermute(sends[1], "dp", behind)
        return first, second

    sends = (part(size - 1, 0), part(1, 1))
    for step in range(size - 1):
        first, second = pass_on(sends)
        sends = (
            first + part(2 * size - 2 - step, 0),
            second + part(2 + step, 1),
        )
    wholes = [values[:, low:high] for low, high in zip(edges, edges[1:])]

    def put(block, side, piece):
        for place, (low, high) in enumerate(zip(edges, edges[1:])):
            wholes[place] = lax.dynamic_update_slice_in_dim(
                wholes[place], piece[:, low:high], start_of(block, side), 0
            )

    put(0, 0, sends[0])
    put(0, 1, sends[1])
    for step in range(size - 1):
        sends = pass_on(sends)
        put(2 * size - 1 - step, 0, sends[0])
        put(1 + step, 1, sends[1])
    return wholes


def join_heads(stack):
    return jnp.swapaxes(stack, 0, 1).reshape(stack.shape[1], -1)


def body(
    tokens,
    out_grad,
    first_gain,
    query_weight,
    key_weight,
    value_weight,
    gate_weight,
    beta_weight,
    decay_weight,
    query_filter,
    key_filter,
    value_filter,
    decay_log,
    decay_bias,
    mixer_gain,
    out_weight,
    second_gain,
    ffn_gate_weight,
    ffn_up_weight,
    ffn_down_weight,
):
    heads = query_weight.shape[1] // DK
    count = tokens.shape[0]
    filters = tuple(
        taps.astype(jnp.float32) for taps in (query_filter, key_filter, value_filter)
    )
    small_weight = jnp.concatenate([beta_weight, decay_weight], 1)
    small_weight = jnp.pad(small_weight, ((0, 0), (0, 128 - 2 * heads)))
    rows = jnp.stack([decay_bias, jnp.exp(decay_log)])
    rows = jnp.pad(rows, ((0, 6), (heads, 128 - 2 * heads)))

    first_normed, pull_first, operands, kept, mixer_out, inputs = [], [], [], [], [], []
    opened = []
    for index in range(count):
        inputs.append(tokens[index].astype(jnp.float32))
        first_float, pull = jax.vjp(root_norm, inputs[index], first_gain)
        pull_first.append(pull)
        normed = first_float.astype(jnp.bfloat16)
        first_normed.append(normed)
        raws = [
            matmul(normed, weight)
            for weight in (query_weight, key_weight, value_weight, gate_weight, small_weight)
        ]
        operands.append((*raws, rows, *filters, mixer_gain))
        out, *saved = mixer_forward(*operands[index])
        mixer_out.append(out)
        kept.append(saved)
        opened.append(open_tensor(against_cols(out, out_weight)))
    middle, outputs, hidden, second_normed = [], [], [], []
    partials, pull_seconds = [], []
    gate_back, up_back, middle_grad, mixer_back, grad_second = [], [], [], [], []
    for index in range(count):
        mixer_sum = close_tensor(opened[index])
        if index:
            mixer_sum = after(mixer_sum, second_partial)
        middle.append(inputs[index] + mixer_sum)
        second_float, pull_second = jax.vjp(root_norm, middle[index], second_gain)
        second_normed.append(second_float.astype(jnp.bfloat16))
        ffn_gate = matmul(second_normed[index], ffn_gate_weight)
        ffn_up = matmul(second_normed[index], ffn_up_weight)
        hidden_float, pull_swiglu = jax.vjp(swiglu, ffn_gate, ffn_up)
        hidden.append(hidden_float.astype(jnp.bfloat16))
        hidden_grad = matmul(out_grad[index], ffn_down_weight)
        gate_grad, up_grad = pull_swiglu(hidden_grad)
        gate_back.append(gate_grad.astype(jnp.bfloat16))
        up_back.append(up_grad.astype(jnp.bfloat16))
        second_partial = against_cols(gate_back[index], ffn_gate_weight) + against_cols(
            up_back[index], ffn_up_weight
        )
        partials.append(second_partial)
        pull_seconds.append(pull_second)
    for index in range(count):
        second_grad = sum_tensor(partials[index])
        second_grad = after(second_grad, second_normed[-1], *mixer_back[:index])
        middle_part, part = pull_seconds[index](second_grad)
        grad_second.append(part)
        middle_grad.append(out_grad[index].astype(jnp.float32) + middle_part)
        mixer_back.append(middle_grad[index].astype(jnp.bfloat16))

    def joined(pieces):
        return jnp.concatenate(pieces, 0)

    def dp(values, cuts=()):
        return sum_ring(values, cuts)

    ffn_back = out_grad.reshape(-1, out_grad.shape[-1])
    normed = joined(second_normed)
    grad_down = dp(against_rows(joined(hidden), ffn_back))[0].T
    both_back = joined([jnp.concatenate(pair, 1) for pair in zip(gate_back, up_back)])
    pair = dp(against_rows(both_back, normed))[0]
    grad_fgate, grad_fup = [piece.T for piece in jnp.split(pair, 2, 0)]
    grad_out = dp(against_rows(joined(mixer_back), joined(mixer_out)))[0]

    backs, taps_back = [], []
    gain_back, input_grads, grad_first = [], [], []
    for index in range(count):
        outnorm_grad = matmul(mixer_back[index], out_weight)
        result = mixer_backward(operands[index], kept[index], outnorm_grad)
        query_back, key_back, value_back, gate_mix, small_grad, *taps, gain_part = result
        backs.append((query_back, key_back, value_back, gate_mix, small_grad))
        taps_back.append([join_heads(piece) for piece in taps])
        gain_back.append(gain_part[0])
    weights = (query_weight, key_weight, value_weight, gate_weight, small_weight)
    normed = joined(first_normed)
    pieces = [joined([back[place] for back in backs]) for place in range(5)]
    small_sums = jnp.sum(pieces[4], 0)
    grad_gate = dp(against_rows(normed, pieces[3]))[0]
    grad_value = dp(against_rows(normed, pieces[2]))[0]
    grad_query, grad_key = dp(
        against_rows(normed, jnp.concatenate(pieces[:2], 1)), (query_weight.shape[1],)
    )
    for index in range(count):
        share = against_cols(after(hidden[index], backs[-1][4]), ffn_down_weight)
        ffn_sum = sum_tensor(share)
        outputs.append((middle[index] + ffn_sum).astype(jnp.bfloat16))
    grad_small = against_rows(normed, pieces[4].astype(jnp.bfloat16))
    for index in range(count):
        first_partial = against_cols(backs[index][4].astype(jnp.bfloat16), small_weight)
        for place in range(4):
            first_partial = first_partial + against_cols(backs[index][place], weights[place])
        first_grad = sum_tensor(first_partial)
        first_grad = after(first_grad, first_normed[-1], mixer_back[-1], *grad_first[:index])
        input_part, part = pull_first[index](first_grad)
        grad_first.append(part)
        input_grads.append((middle_grad[index] + input_part).astype(jnp.bfloat16))

    def total(parts):
        whole = parts[0]
        for part in parts[1:]:
            whole = whole + part
        return whole

    small = [
        grad_small[:, :heads],
        grad_small[:, heads : 2 * heads],
        total([taps[0] for taps in taps_back]),
        total([taps[1] for taps in taps_back]),
        total([taps[2] for taps in taps_back]),
        small_sums[2 * heads : 3 * heads],
        small_sums[heads : 2 * heads],
        sum_whole(total(gain_back), "tensor"),
        total(grad_first),
        total(grad_second),
    ]
    flat = jnp.concatenate([piece.reshape(-1) for piece in small])
    flat = jnp.pad(flat, (0, -flat.shape[0] % 1024)).reshape(-1, 128)
    flat = sum_whole(flat, "dp").reshape(-1)
    parts = []
    position = 0
    for piece in small:
        parts.append(flat[position : position + piece.size].reshape(piece.shape))
        position = position + piece.size
    return (
        jnp.stack(outputs),
        jnp.stack(input_grads),
        parts[8],
        grad_query,
        grad_key,
        grad_value,
        grad_gate,
        parts[0],
        parts[1],
        parts[2],
        parts[3],
        parts[4],
        parts[5],
        parts[6],
        parts[7],
        grad_out,
        parts[9],
        grad_fgate,
        grad_fup,
        grad_down,
    )


def solution(mesh):
    in_specs = (
        P("dp", None, None),
        P("dp", None, None),
        P(),
        P(None, "tensor"),
        P(None, "tensor"),
        P(None, "tensor"),
        P(None, "tensor"),
        P(None, "tensor"),
        P(None, "tensor"),
        P(None, "tensor"),
        P(None, "tensor"),
        P(None, "tensor"),
        P("tensor"),
        P("tensor"),
        P(),
        P(None, "tensor"),
        P(),
        P(None, "tensor"),
        P(None, "tensor"),
        P(None, "tensor"),
    )
    out_specs = (
        P("dp", None, None),
        P("dp", None, None),
        P(),
        P(None, "tensor"),
        P(None, "tensor"),
        P(None, "tensor"),
        P(None, "tensor"),
        P(None, "tensor"),
        P(None, "tensor"),
        P(None, "tensor"),
        P(None, "tensor"),
        P(None, "tensor"),
        P("tensor"),
        P("tensor"),
        P(),
        P(None, "tensor"),
        P(),
        P(None, "tensor"),
        P(None, "tensor"),
        P(None, "tensor"),
    )

    return jax.shard_map(body, mesh=mesh, in_specs=in_specs, out_specs=out_specs, check_vma=False)
```
